256 devices in a mesh: ctx: 32 (over x, y, core), head: 8 (over z).
Axes of the slice: x: 4, y: 4, z: 8, core: 2. Of those that a mesh axis runs over, the one named last changes fastest.
Arguments:
- queries: bfloat16 [8192, 2048], P(('ctx', 'head')), may hold values from -6 to 6
- keys: bfloat16 [8192, 2048], P(('ctx', 'head')), may hold values from -6 to 6
- values: bfloat16 [8192, 2048], P(('ctx', 'head')), may hold values from -6 to 6
- ridge: float32 [16], P('head'), may hold values from 0.5 to 4
- gain: float32 [2048], P('head'), may hold values from 0.5 to 1.5
Outputs:
- mixed: bfloat16 [8192, 2048], P(('ctx', 'head'))
The draws below stay inside these ranges and needn't reach their ends.
All inputs are finite; a program needn't handle non-finite values.
Results may differ from the reference program's by a relative error of at most 0.0015.
Values may be sent and summed in bfloat16 or wider, within the bound.
No kernel may reach another device: no remote copies, remote signals or barrier semaphores. Data moves between devices by JAX's collectives and lax.ppermute only.
A program may use at most 64 MiB of HBM per device.

```python
import math
import jax
import jax.numpy as jnp
from jax import lax

HEADS = 16
DH = 128
CTX_TOK = 256
ITERS = 4
TOKENS = 8192
N_CTX = 32


def draw_keys(key, part):
    base_key = jax.random.fold_in(key, 4711)
    noise_key, floor_key, mixing_key = jax.random.split(base_key, 3)
    floors = jnp.exp(jax.random.uniform(floor_key, (HEADS, 1), jnp.float32, math.log(0.003), math.log(0.03)))
    ladder = jnp.arange(DH, dtype=jnp.float32) / (DH - 1)
    spectrum = jnp.exp(ladder[None, :] * jnp.log(floors))
    mixing = jax.random.normal(mixing_key, (HEADS, DH, DH), jnp.float32) / math.sqrt(DH)
    source = jax.random.normal(noise_key, (TOKENS, HEADS, DH), jnp.float32)
    shaped = jnp.einsum('thd,hde->the', source * spectrum[None], mixing)
    shaped = shaped * lax_rsqrt_mean(spectrum)[None, :, None]
    shaped = jnp.clip(shaped, -6.0, 6.0)
    return shaped.reshape(TOKENS, HEADS * DH).astype(jnp.bfloat16)


def lax_rsqrt_mean(spectrum):
    return 1.0 / jnp.sqrt(jnp.mean(spectrum * spectrum, -1))


def block_levels(key, dims, cuts, smallest, high):
    loudness, own = 1.0, jax.random.fold_in(key, 6)
    for dim, parts in cuts:
        steps = jnp.exp(jax.random.uniform(jax.random.fold_in(own, dim), (parts,), jnp.float32, smallest / len(cuts), high / len(cuts)))
        loudness = loudness * jnp.repeat(steps, dims[dim] // parts).reshape([-1 if axis == dim else 1 for axis in range(len(dims))])
    return loudness


def scatter_about(stream_key, shape, scale, bound, cuts=(), held_as=jnp.bfloat16):
    entries = jax.random.normal(stream_key, shape, jnp.float32) * scale
    if len(cuts) > 0:
        entries = block_levels(stream_key, shape, cuts, -0.22, 0.18) * entries
    return jnp.clip(entries, min=-bound, max=bound).astype(held_as)


def setup_inputs(seed: int = 0) -> dict:
    key_list = jax.random.split(jax.random.key(seed), 6)
    return {
        "queries": scatter_about(key_list[0], (TOKENS, HEADS * DH), 1.0, 6.0, ((0, 256),)),
        "keys": draw_keys(jax.random.fold_in(key_list[5], 71), 0),
        "values": scatter_about(key_list[2], (TOKENS, HEADS * DH), 1.0, 6.0, ((0, 256),)),
        "ridge": jnp.clip(jnp.exp(math.log(4.0) - 2.0794415 * jax.random.uniform(key_list[3], (HEADS,), jnp.float32) ** block_levels(key_list[3], (HEADS,), ((0, 8),), -0.2, 0.2)), 0.5, 4.0),
        "gain": jnp.clip(1.0 + 0.1 * jax.random.normal(key_list[4], (HEADS * DH,), jnp.float32), 0.5, 1.5),
    }


EPS = 1e-06
HIGH = lax.Precision.HIGHEST

def unit_rows(matrix):
    return matrix * lax.rsqrt(lax.optimization_barrier(jnp.sum(matrix * matrix, -1, keepdims=True)) + EPS)

def solve_block(query_blk, key_blk, value_blk, key_state, value_state, strength):
    causal = jnp.tril(jnp.ones((CTX_TOK, CTX_TOK), jnp.float32))

    def apply_op(direction):
        scores = jnp.dot(direction, key_blk.T, precision=HIGH) * causal
        return jnp.dot(scores, key_blk, precision=HIGH) + jnp.dot(direction, key_state, precision=HIGH) + strength * direction
    answer = jnp.zeros_like(query_blk)
    resid = query_blk
    direction = query_blk
    rr_now = lax.optimization_barrier(jnp.sum(resid * resid, -1, keepdims=True))
    for turn in range(ITERS):
        image = apply_op(direction)
        alpha = rr_now / (lax.optimization_barrier(jnp.sum(direction * image, -1, keepdims=True)) + EPS)
        answer = answer + alpha * direction
        resid = resid - alpha * image
        rr_next = lax.optimization_barrier(jnp.sum(resid * resid, -1, keepdims=True))
        direction = resid + rr_next / (rr_now + EPS) * direction
        rr_now = rr_next
    scores = jnp.dot(answer, key_blk.T, precision=HIGH) * causal
    return jnp.dot(scores, value_blk, precision=HIGH) + jnp.dot(answer, value_state.T, precision=HIGH)

def reference(queries, keys, values, ridge, gain):

    def to_heads(matrix):
        return matrix.astype(jnp.float32).reshape(TOKENS, HEADS, DH).transpose(1, 0, 2).reshape(HEADS, N_CTX, CTX_TOK, DH)

    def one_head(items):
        query_h, key_h, value_h, strength = items
        query_h = unit_rows(query_h)
        key_h = unit_rows(key_h)

        def advance(carry, blocks):
            key_state, value_state = carry
            query_blk, key_blk, value_blk = blocks
            result = solve_block(query_blk, key_blk, value_blk, key_state, value_state, strength)
            key_state = key_state + jnp.dot(key_blk.T, key_blk, precision=HIGH)
            value_state = value_state + jnp.dot(value_blk.T, key_blk, precision=HIGH)
            return ((key_state, value_state), result)
        start = (jnp.zeros((DH, DH), jnp.float32), jnp.zeros((DH, DH), jnp.float32))
        carry_end, results = lax.scan(advance, start, (query_h, key_h, value_h))
        return results
    readout = lax.map(one_head, (to_heads(queries), to_heads(keys), to_heads(values), ridge))
    readout = readout.reshape(HEADS, TOKENS, DH)
    scale = lax.rsqrt(lax.optimization_barrier(jnp.mean(readout * readout, -1, keepdims=True)) + EPS)
    normed = readout * scale * gain.reshape(HEADS, 1, DH)
    return normed.transpose(1, 0, 2).reshape(TOKENS, HEADS * DH).astype(jnp.bfloat16)
```

```python
import jax
import jax.numpy as jnp
from jax import lax
from jax.sharding import Mesh
from jax.sharding import PartitionSpec as P

ITERS = 4
CTX_HEAD = ("x", "y", "core", "head")
PEERS = ("head", "core")


EPS = 1e-06
HIGH = lax.Precision.HIGHEST


def unit_rows(matrix):
    return matrix * lax.rsqrt(jnp.sum(matrix * matrix, -1, keepdims=True) + EPS)


def earlier_states(local):
    x, y = lax.axis_index("x"), lax.axis_index("y")
    n_x, n_y = lax.axis_size("x"), lax.axis_size("y")
    slots = (n_x,) + local.shape
    arrived = lax.all_to_all(jnp.broadcast_to(local, slots), "x", 0, 0, tiled=True)
    ranks = jnp.arange(n_x).reshape(n_x, 1, 1)
    column = jnp.sum(jnp.where(ranks < x, arrived, 0.0), 0)
    ranks = jnp.arange(n_y).reshape(n_y, 1, 1)
    outgoing = column + jnp.where(ranks > y, local, 0.0)
    return jnp.sum(lax.all_to_all(outgoing, "y", 0, 0, tiled=True), 0)


def on_device(queries, keys, values, ridge, gain):
    rows, columns = queries.shape
    peers = lax.axis_size("head") * lax.axis_size("core")
    width = columns // peers
    packed = jnp.stack([queries, keys, values], 0).reshape(3, rows, peers, width)
    packed = packed.transpose(2, 0, 1, 3)
    arrived = lax.all_to_all(packed, PEERS, 0, 0, tiled=True)
    arrived = arrived.reshape(peers // 2, 2, 3, rows, width).transpose(2, 1, 0, 3, 4)
    arrived = arrived.reshape(3, 2, rows * peers // 2, width).astype(jnp.float32)
    core = lax.axis_index("core")
    strength = lax.dynamic_slice(ridge, (core,), (1,)).reshape(1, 1, 1)
    gain_h = lax.dynamic_slice(gain.reshape(2, width), (core, 0), (1, width)).reshape(1, 1, width)

    query_h = unit_rows(arrived[0])
    key_h = unit_rows(arrived[1])
    value_h = arrived[2]
    tokens = query_h.shape[1]
    both = jnp.concatenate([key_h, value_h], -1)
    local = jnp.einsum("hld,hle->hed", key_h, both, precision=HIGH)
    before = earlier_states(local[0] + local[1])
    state = jnp.stack([before, before + local[0]], 0)
    key_state = state[:, :width]
    value_state = state[:, width:]
    causal = jnp.tril(jnp.ones((tokens, tokens), jnp.float32))
    answer = jnp.zeros_like(query_h)
    resid = query_h
    direction = query_h
    rr_now = jnp.sum(resid * resid, -1, keepdims=True)
    for turn in range(ITERS):
        apply_scores = jnp.einsum("htd,hid->hti", direction, key_h, precision=HIGH) * causal
        image = (
            jnp.einsum("hti,hid->htd", apply_scores, key_h, precision=HIGH)
            + jnp.einsum("htd,hde->hte", direction, key_state, precision=HIGH)
            + strength * direction
        )
        alpha = rr_now / (jnp.sum(direction * image, -1, keepdims=True) + EPS)
        answer = answer + alpha * direction
        resid = resid - alpha * image
        rr_next = jnp.sum(resid * resid, -1, keepdims=True)
        direction = resid + rr_next / (rr_now + EPS) * direction
        rr_now = rr_next
    scores = jnp.einsum("htd,hid->hti", answer, key_h, precision=HIGH) * causal
    readout = jnp.einsum("hti,hid->htd", scores, value_h, precision=HIGH) + jnp.einsum(
        "hte,hde->htd", answer, value_state, precision=HIGH
    )
    scale = lax.rsqrt(jnp.mean(readout * readout, -1, keepdims=True) + EPS)
    normed = (readout * scale * gain_h).astype(jnp.bfloat16)
    outgoing = normed.reshape(2, peers // 2, rows, width).transpose(1, 0, 2, 3)
    outgoing = outgoing.reshape(peers, rows, width)
    home = lax.all_to_all(outgoing, PEERS, 0, 0, tiled=True)
    return home.transpose(1, 0, 2).reshape(rows, columns)


def solution(mesh):
    split = Mesh(mesh.devices.reshape(4, 4, 2, mesh.shape["head"]), CTX_HEAD)
    rows = P(CTX_HEAD, None)
    return jax.shard_map(
        on_device,
        mesh=split,
        in_specs=(rows, rows, rows, P("head"), P("head")),
        out_specs=rows,
        check_vma=False,
    )
```

```python
import functools

import jax
import jax.numpy as jnp
from jax import lax
from jax.experimental import pallas as pl
from jax.experimental.pallas import tpu as pltpu
from jax.sharding import Mesh
from jax.sharding import PartitionSpec as P

ITERS = 4
CTX_HEAD = ("x", "y", "core", "head")
PEERS = ("core", "head")
EPS = 1e-06
DH = 128
SUB = 128

VMEM = pl.BlockSpec(memory_space=pltpu.VMEM)
HBM = pl.BlockSpec(memory_space=pltpu.HBM)
SMEM = pl.BlockSpec(memory_space=pltpu.SMEM)
BF = jnp.bfloat16
F32 = jnp.float32
ROOM = pltpu.CompilerParams(vmem_limit_bytes=16 * 2**20)


def pieces(value, count):
    out = []
    for _ in range(count - 1):
        out.append(value.astype(BF))
        value = value - out[-1].astype(F32)
    return out + [value.astype(BF)]


def wide(parts):
    return jnp.concatenate(parts, 1)


def tall(parts):
    return jnp.concatenate(parts, 0)


def dot(a, b):
    return lax.dot_general(a, b, (((1,), (0,)), ((), ())), preferred_element_type=F32)


def tokens_of(arrived_ref, which, sub):
    count = SUB // arrived_ref.shape[2]
    return tall([arrived_ref[sub * count + i, which] for i in range(count)])


def squared_sum(value):
    return jnp.sum(value * value, -1, keepdims=True)


def pack_kernel(
    query_ref, key_ref, value_ref, ridge_ref, gain_ref, out_ref, head_ref, held, flags, *, peers
):
    copies = [
        pltpu.make_async_copy(ref, held.at[which], flags.at[which])
        for which, ref in enumerate((query_ref, key_ref, value_ref))
    ]
    for copy in copies:
        copy.start()
    core = lax.axis_index("core")
    head_ref[...] = jnp.full(head_ref.shape, ridge_ref[core], F32)
    head_ref[pl.ds(0, 1), :] = gain_ref[pl.ds(core, 1), :]
    half = peers // 2
    for which, copy in enumerate(copies):
        copy.wait()
        for peer in range(peers):
            head = 2 * (peer % half) + peer // half
            out_ref[peer, which] = held[which, :, head * DH : (head + 1) * DH]


def states_kernel(arrived_ref, before_ref, total_ref, *, subs):
    total = None
    for sub in range(subs):
        key = tokens_of(arrived_ref, 1, sub)
        value = tokens_of(arrived_ref, 2, sub)
        key_f = key.astype(F32)
        unit = lax.rsqrt(squared_sum(key_f) + EPS)
        right = wide([key_f * (unit * unit), value.astype(F32) * unit])
        key_t = key_f.T.astype(BF)
        state = dot(wide([key_t, key_t]), tall(pieces(right, 2)))
        total = state if total is None else total + state
        if sub + 1 < subs:
            before_ref[sub] = total
    total_ref[...] = total


def from_others(index, own, others, steps):
    total, earlier = own, None
    for step, ref in zip(steps, others):
        value = ref[...]
        total = total + value
        part = jnp.where(index >= step, value, 0.0)
        earlier = part if earlier is None else earlier + part
    return total, earlier


def row_kernel(own_ref, *refs, steps):
    total_ref, earlier_ref = refs[-2:]
    total, earlier = from_others(
        lax.axis_index("y"), own_ref[...], refs[:-2], steps
    )
    total_ref[...] = total
    earlier_ref[...] = earlier


def solve_kernel(head_ref, arrived_ref, before_ref, earlier_ref, *refs, subs, steps):
    out_ref = refs[-1]
    gain, strength = head_ref[0:1, :], head_ref[1:2, :]
    earlier = earlier_ref[...]
    _, rows_before = from_others(lax.axis_index("x"), earlier, refs[:-1], steps)
    base = earlier + rows_before
    row = lax.broadcasted_iota(jnp.int32, (SUB, SUB), 0)
    column = lax.broadcasted_iota(jnp.int32, (SUB, SUB), 1)
    causal = column <= row

    every = range(subs)
    keys, key_pair, operator, low_state, weights, units = [], [], [], [], [], []
    value_state = []
    resid, answer, direction, rr_now = [], [], [], []
    for sub in every:
        state = base if sub == 0 else base + before_ref[sub - 1]
        key = tokens_of(arrived_ref, 1, sub)
        key_f = key.astype(F32)
        unit_t = lax.rsqrt(jnp.sum((key_f * key_f).T, 0, keepdims=True) + EPS)
        units.append(jnp.where(causal, unit_t, 0.0))
        weights.append(jnp.where(causal, unit_t * unit_t, 0.0))
        high, middle, low = pieces(state[:, :DH], 3)
        key_t = key_f.T.astype(BF)
        keys.append(key_t)
        key_pair.append(tall([key, key]))
        operator.append(tall([wide([key_t, high])] * 3))
        low_state.append(tall([wide([middle, low])] * 2))
        value_state.append(state[:, DH:])
        query = tokens_of(arrived_ref, 0, sub).astype(F32)
        query = query * lax.rsqrt(squared_sum(query) + EPS)
        resid.append(query)
        direction.append(query)
        answer.append(None)
        rr_now.append(squared_sum(query))
    for turn in range(ITERS):
        parts = [wide(pieces(direction[s], 3)) for s in every]
        first = [dot(parts[s], operator[s]) for s in every]
        rest = [dot(parts[s][:, : 2 * DH], low_state[s]) for s in every]
        scores = [wide(pieces(first[s][:, :SUB] * weights[s], 2)) for s in every]
        image = [
            dot(scores[s], key_pair[s])
            + (first[s][:, SUB:] + (rest[s][:, :DH] + rest[s][:, DH:]))
            + strength * direction[s]
            for s in every
        ]
        for s in every:
            alpha = rr_now[s] / (jnp.sum(direction[s] * image[s], -1, keepdims=True) + EPS)
            step = alpha * direction[s]
            answer[s] = step if turn == 0 else answer[s] + step
            if turn + 1 < ITERS:
                resid[s] = resid[s] - alpha * image[s]
                rr_next = squared_sum(resid[s])
                direction[s] = resid[s] + rr_next / (rr_now[s] + EPS) * direction[s]
                rr_now[s] = rr_next
    rows = out_ref.shape[1]
    count = SUB // rows
    for s in every:
        high, low = pieces(value_state[s], 2)
        parts = wide(pieces(answer[s], 2))
        first = dot(parts, tall([wide([keys[s], high])] * 2))
        scores = wide(pieces(first[:, :SUB] * units[s], 2))
        value = tokens_of(arrived_ref, 2, s)
        readout = dot(scores, tall([value, value]))
        readout = readout + (first[:, SUB:] + dot(parts[:, :DH], low))
        scale = lax.rsqrt(squared_sum(readout) * (1.0 / DH) + EPS)
        normed = (readout * scale * gain).astype(BF)
        for i in range(count):
            out_ref[s * count + i] = normed[i * rows : (i + 1) * rows]


def exchange(value):
    return lax.all_to_all(value, PEERS, 0, 0, tiled=True)


def from_ring(value, axis, steps):
    size = lax.axis_size(axis)
    return [
        lax.ppermute(value, axis, [(i, (i + step) % size) for i in range(size)]) for step in steps
    ]


def ring_steps(size):
    return sorted(range(1, size), key=lambda step: min(step, size - step))


def on_device(queries, keys, values, ridge, gain):
    rows, columns = queries.shape
    half = lax.axis_size("head")
    peers = 2 * half
    n_x, n_y = lax.axis_size("x"), lax.axis_size("y")
    subs = peers * rows // SUB
    steps_x, steps_y = ring_steps(n_x), ring_steps(n_y)
    packed, head = pl.pallas_call(
        functools.partial(pack_kernel, peers=peers),
        out_shape=(
            jax.ShapeDtypeStruct((peers, 3, rows, DH), BF),
            jax.ShapeDtypeStruct((8, DH), F32),
        ),
        in_specs=[HBM, HBM, HBM, SMEM, VMEM],
        out_specs=(VMEM, VMEM),
        scratch_shapes=[
            pltpu.VMEM((3, rows, columns), BF),
            pltpu.SemaphoreType.DMA((3,)),
        ],
        compiler_params=ROOM,
        name="pack",
    )(queries, keys, values, ridge, gain.reshape(2, DH))
    arrived = exchange(packed)

    state = jax.ShapeDtypeStruct((DH, 2 * DH), F32)
    before, own = pl.pallas_call(
        functools.partial(states_kernel, subs=subs),
        out_shape=(jax.ShapeDtypeStruct((subs - 1,) + state.shape, F32), state),
        in_specs=[VMEM],
        out_specs=(VMEM, VMEM),
        compiler_params=ROOM,
        name="states",
    )(arrived)
    total, earlier = pl.pallas_call(
        functools.partial(row_kernel, steps=steps_y),
        out_shape=(state, state),
        in_specs=[VMEM] * n_y,
        out_specs=(VMEM, VMEM),
        compiler_params=ROOM,
        name="row",
    )(own, *from_ring(own, "y", steps_y))
    outgoing = pl.pallas_call(
        functools.partial(solve_kernel, subs=subs, steps=steps_x),
        out_shape=jax.ShapeDtypeStruct((peers, rows, DH), BF),
        in_specs=[VMEM] * (3 + n_x),
        out_specs=VMEM,
        compiler_params=ROOM,
        name="solve",
    )(head, arrived, before, earlier, *from_ring(total, "x", steps_x))
    home = exchange(outgoing).reshape(2, half, rows, DH)
    return home.transpose(2, 1, 0, 3).reshape(rows, columns)


def solution(mesh):
    split = Mesh(mesh.devices.reshape(4, 4, 2, mesh.shape["head"]), CTX_HEAD)
    rows = P(CTX_HEAD, None)
    return jax.shard_map(
        on_device,
        mesh=split,
        in_specs=(rows, rows, rows, P("head"), P("head")),
        out_specs=rows,
        check_vma=False,
    )
```

```python
import functools

import jax
import jax.numpy as jnp
from jax import lax
from jax.experimental import pallas as pl
from jax.experimental.pallas import tpu as pltpu
from jax.sharding import Mesh
from jax.sharding import PartitionSpec as P

ITERS = 4
CTX_HEAD = ("x", "y", "core", "head")
PEERS = ("core", "head")
EPS = 1e-06
DH = 128
SUB = 128

VMEM = pl.BlockSpec(memory_space=pltpu.VMEM)
HBM = pl.BlockSpec(memory_space=pltpu.HBM)
SMEM = pl.BlockSpec(memory_space=pltpu.SMEM)
BF = jnp.bfloat16
F32 = jnp.float32
ROOM = pltpu.CompilerParams(vmem_limit_bytes=16 * 2**20)


def pieces(value, count):
    out = []
    for _ in range(count - 1):
        out.append(value.astype(BF))
        value = value - out[-1].astype(F32)
    return out + [value.astype(BF)]


def wide(parts):
    return jnp.concatenate(parts, 1)


def tall(parts):
    return jnp.concatenate(parts, 0)


def dot(a, b):
    return lax.dot_general(a, b, (((1,), (0,)), ((), ())), preferred_element_type=F32)


def tokens_of(arrived_ref, which, sub):
    count = SUB // arrived_ref.shape[2]
    return tall([arrived_ref[sub * count + i, which] for i in range(count)])


def squared_sum(value):
    return jnp.sum(value * value, -1, keepdims=True)


def pack_kernel(
    query_ref, key_ref, value_ref, ridge_ref, gain_ref, out_ref, head_ref,
    held, ridges, gains, flags, *, peers
):
    half = peers // 2
    copies = [
        pltpu.make_async_copy(source, target, flags.at[i])
        for i, (source, target) in enumerate(
            (
                (query_ref, held.at[0]),
                (key_ref, held.at[1]),
                (value_ref, held.at[2]),
                (ridge_ref, ridges),
                (gain_ref, gains),
            )
        )
    ]
    for copy in copies:
        copy.start()
    for i in range(3):
        copies[i].wait()
        for peer in range(peers):
            head = 2 * (peer % half) + peer // half
            out_ref[peer, i] = held[i, :, head * DH : (head + 1) * DH]
    copies[3].wait()
    copies[4].wait()
    core = lax.axis_index("core")
    head_ref[...] = jnp.full(head_ref.shape, ridges[core], F32)
    head_ref[pl.ds(0, 1), :] = gains[pl.ds(core, 1), :]


def unpack_kernel(arrived_ref, out_ref):
    peers = arrived_ref.shape[0]
    half = peers // 2
    for peer in range(peers):
        head = 2 * (peer % half) + peer // half
        out_ref[:, head * DH : (head + 1) * DH] = arrived_ref[peer]


def states_kernel(arrived_ref, before_ref, total_ref, *, subs):
    total = None
    for sub in range(subs):
        key = tokens_of(arrived_ref, 1, sub)
        value = tokens_of(arrived_ref, 2, sub)
        key_f = key.astype(F32)
        unit = lax.rsqrt(squared_sum(key_f) + EPS)
        right = wide([key_f * (unit * unit), value.astype(F32) * unit])
        key_t = key_f.T.astype(BF)
        state = dot(wide([key_t, key_t]), tall(pieces(right, 2)))
        total = state if total is None else total + state
        if sub + 1 < subs:
            before_ref[sub] = total
    total_ref[...] = total


def from_others(index, own, others, steps):
    total, earlier = own, None
    for step, ref in zip(steps, others):
        value = ref[...]
        total = total + value
        part = jnp.where(index >= step, value, 0.0)
        earlier = part if earlier is None else earlier + part
    return total, earlier


def row_kernel(own_ref, *refs, steps):
    total_ref, earlier_ref = refs[-2:]
    total, earlier = from_others(
        lax.axis_index("y"), own_ref[...], refs[:-2], steps
    )
    total_ref[...] = total
    earlier_ref[...] = earlier


def solve_kernel(head_ref, arrived_ref, before_ref, earlier_ref, *refs, subs, steps):
    out_ref = refs[-1]
    gain, strength = head_ref[0:1, :], head_ref[1:2, :]
    earlier = earlier_ref[...]
    _, rows_before = from_others(lax.axis_index("x"), earlier, refs[:-1], steps)
    base = earlier + rows_before
    row = lax.broadcasted_iota(jnp.int32, (SUB, SUB), 0)
    column = lax.broadcasted_iota(jnp.int32, (SUB, SUB), 1)
    causal = column <= row

    every = range(subs)
    keys, key_pair, operator, low_state, weights, units = [], [], [], [], [], []
    value_state = []
    resid, answer, direction, rr_now = [], [], [], []
    for sub in every:
        state = base if sub == 0 else base + before_ref[sub - 1]
        key = tokens_of(arrived_ref, 1, sub)
        key_f = key.astype(F32)
        unit_t = lax.rsqrt(jnp.sum((key_f * key_f).T, 0, keepdims=True) + EPS)
        units.append(jnp.where(causal, unit_t, 0.0))
        weights.append(jnp.where(causal, unit_t * unit_t, 0.0))
        high, middle, low = pieces(state[:, :DH], 3)
        key_t = key_f.T.astype(BF)
        keys.append(key_t)
        key_pair.append(tall([key, key]))
        operator.append(tall([wide([key_t, high])] * 3))
        low_state.append(tall([wide([middle, low])] * 2))
        value_state.append(state[:, DH:])
        query = tokens_of(arrived_ref, 0, sub).astype(F32)
        query = query * lax.rsqrt(squared_sum(query) + EPS)
        resid.append(query)
        direction.append(query)
        answer.append(None)
        rr_now.append(squared_sum(query))
    for turn in range(ITERS):
        parts = [wide(pieces(direction[s], 3)) for s in every]
        first = [dot(parts[s], operator[s]) for s in every]
        rest = [dot(parts[s][:, : 2 * DH], low_state[s]) for s in every]
        scores = [wide(pieces(first[s][:, :SUB] * weights[s], 2)) for s in every]
        image = [
            dot(scores[s], key_pair[s])
            + (first[s][:, SUB:] + (rest[s][:, :DH] + rest[s][:, DH:]))
            + strength * direction[s]
            for s in every
        ]
        for s in every:
            alpha = rr_now[s] / (jnp.sum(direction[s] * image[s], -1, keepdims=True) + EPS)
            step = alpha * direction[s]
            answer[s] = step if turn == 0 else answer[s] + step
            if turn + 1 < ITERS:
                resid[s] = resid[s] - alpha * image[s]
                rr_next = squared_sum(resid[s])
                direction[s] = resid[s] + rr_next / (rr_now[s] + EPS) * direction[s]
                rr_now[s] = rr_next
    rows = out_ref.shape[1]
    count = SUB // rows
    for s in every:
        high, low = pieces(value_state[s], 2)
        parts = wide(pieces(answer[s], 2))
        first = dot(parts, tall([wide([keys[s], high])] * 2))
        scores = wide(pieces(first[:, :SUB] * units[s], 2))
        value = tokens_of(arrived_ref, 2, s)
        readout = dot(scores, tall([value, value]))
        readout = readout + (first[:, SUB:] + dot(parts[:, :DH], low))
        scale = lax.rsqrt(squared_sum(readout) * (1.0 / DH) + EPS)
        normed = (readout * scale * gain).astype(BF)
        for i in range(count):
            out_ref[s * count + i] = normed[i * rows : (i + 1) * rows]


def exchange(value):
    return lax.all_to_all(value, PEERS, 0, 0, tiled=True)


def from_ring(value, axis, steps):
    size = lax.axis_size(axis)
    return [
        lax.ppermute(value, axis, [(i, (i + step) % size) for i in range(size)]) for step in steps
    ]


def ring_steps(size):
    return [size - 1] + list(range(1, size - 1))


def in_hbm(value):
    return pltpu.with_memory_space_constraint(value, pltpu.HBM)


def on_device(queries, keys, values, ridge, gain):
    rows, columns = queries.shape
    half = lax.axis_size("head")
    peers = 2 * half
    n_x, n_y = lax.axis_size("x"), lax.axis_size("y")
    subs = peers * rows // SUB
    steps_x, steps_y = ring_steps(n_x), ring_steps(n_y)
    packed, head = pl.pallas_call(
        functools.partial(pack_kernel, peers=peers),
        out_shape=(
            jax.ShapeDtypeStruct((peers, 3, rows, DH), BF),
            jax.ShapeDtypeStruct((8, DH), F32),
        ),
        in_specs=[HBM] * 5,
        out_specs=(VMEM, VMEM),
        scratch_shapes=[
            pltpu.VMEM((3, rows, columns), BF),
            pltpu.SMEM((2,), F32),
            pltpu.VMEM((2, DH), F32),
            pltpu.SemaphoreType.DMA((5,)),
        ],
        compiler_params=ROOM,
        name="pack",
    )(*map(in_hbm, (queries, keys, values, ridge, gain.reshape(2, DH))))
    arrived = exchange(packed)

    state = jax.ShapeDtypeStruct((DH, 2 * DH), F32)
    before, own = pl.pallas_call(
        functools.partial(states_kernel, subs=subs),
        out_shape=(jax.ShapeDtypeStruct((subs - 1,) + state.shape, F32), state),
        in_specs=[VMEM],
        out_specs=(VMEM, VMEM),
        compiler_params=ROOM,
        name="states",
    )(arrived)
    total, earlier = pl.pallas_call(
        functools.partial(row_kernel, steps=steps_y),
        out_shape=(state, state),
        in_specs=[VMEM] * n_y,
        out_specs=(VMEM, VMEM),
        compiler_params=ROOM,
        name="row",
    )(own, *from_ring(own, "y", steps_y))
    outgoing = pl.pallas_call(
        functools.partial(solve_kernel, subs=subs, steps=steps_x),
        out_shape=jax.ShapeDtypeStruct((peers, rows, DH), BF),
        in_specs=[VMEM] * (3 + n_x),
        out_specs=VMEM,
        compiler_params=ROOM,
        name="solve",
    )(head, arrived, before, earlier, *from_ring(total, "x", steps_x))
    return pl.pallas_call(
        unpack_kernel,
        out_shape=jax.ShapeDtypeStruct((rows, columns), BF),
        in_specs=[VMEM],
        out_specs=VMEM,
        compiler_params=ROOM,
        name="unpack",
    )(exchange(outgoing))


def solution(mesh):
    split = Mesh(mesh.devices.reshape(4, 4, 2, mesh.shape["head"]), CTX_HEAD)
    rows = P(CTX_HEAD, None)
    return jax.shard_map(
        on_device,
        mesh=split,
        in_specs=(rows, rows, rows, P("head"), P("head")),
        out_specs=rows,
        check_vma=False,
    )
```

```python
import functools

import jax
import jax.numpy as jnp
from jax import lax
from jax.experimental import pallas as pl
from jax.experimental.pallas import tpu as pltpu
from jax.sharding import Mesh
from jax.sharding import PartitionSpec as P

ITERS = 4
CTX_HEAD = ("x", "y", "core", "head")
PEERS = ("core", "head")
EPS = 1e-06
DH = 128
SUB = 128
HALF = DH // 2

VMEM = pl.BlockSpec(memory_space=pltpu.VMEM)
HBM = pl.BlockSpec(memory_space=pltpu.HBM)
SMEM = pl.BlockSpec(memory_space=pltpu.SMEM)
BF = jnp.bfloat16
F32 = jnp.float32
ROOM = pltpu.CompilerParams(vmem_limit_bytes=16 * 2**20)


def pieces(value, count):
    out = []
    for _ in range(count - 1):
        out.append(value.astype(BF))
        value = value - out[-1].astype(F32)
    return out + [value.astype(BF)]


def wide(parts):
    return jnp.concatenate(parts, 1)


def tall(parts):
    return jnp.concatenate(parts, 0)


def dot(a, b):
    return lax.dot_general(a, b, (((1,), (0,)), ((), ())), preferred_element_type=F32)


def tokens_of(arrived_ref, which, sub):
    count = SUB // arrived_ref.shape[2]
    return tall([arrived_ref[sub * count + i, which] for i in range(count)])


def squared_sum(value):
    return jnp.sum(value * value, -1, keepdims=True)


def pack_kernel(
    query_ref, key_ref, value_ref, ridge_ref, gain_ref, out_ref, head_ref,
    held, ridges, gains, flags, *, peers
):
    half = peers // 2
    copies = [
        pltpu.make_async_copy(source, target, flags.at[i])
        for i, (source, target) in enumerate(
            (
                (query_ref, held.at[0]),
                (key_ref, held.at[1]),
                (value_ref, held.at[2]),
                (ridge_ref, ridges),
                (gain_ref, gains),
            )
        )
    ]
    for copy in copies:
        copy.start()
    for i in range(3):
        copies[i].wait()
        for peer in range(peers):
            head = 2 * (peer % half) + peer // half
            out_ref[peer, i] = held[i, :, head * DH : (head + 1) * DH]
    copies[3].wait()
    copies[4].wait()
    core = lax.axis_index("core")
    head_ref[...] = jnp.full(head_ref.shape, ridges[core], F32)
    head_ref[pl.ds(0, 1), :] = gains[pl.ds(core, 1), :]


def unpack_kernel(arrived_ref, out_ref):
    peers = arrived_ref.shape[0]
    half = peers // 2
    for peer in range(peers):
        head = 2 * (peer % half) + peer // half
        out_ref[:, head * DH : (head + 1) * DH] = arrived_ref[peer]


def without_mirror(state):
    key_state, value_state = state[:, :DH], state[:, DH:]
    corner = key_state[HALF:, HALF:]
    return tall(
        [value_state, key_state[:HALF], wide([corner[: HALF // 2], corner[HALF // 2 :]])]
    )


def with_mirror(rows):
    upper, corner = rows[DH : DH + HALF], rows[DH + HALF :]
    corner = tall([corner[:, :HALF], corner[:, HALF:]])
    lower = wide([upper[:, HALF:].T, corner])
    return tall([upper, lower]), rows[:DH]


def states_kernel(arrived_ref, before_ref, total_ref, *, subs):
    total = None
    for sub in range(subs):
        key = tokens_of(arrived_ref, 1, sub)
        value = tokens_of(arrived_ref, 2, sub)
        key_f = key.astype(F32)
        unit = lax.rsqrt(squared_sum(key_f) + EPS)
        right = wide([key_f * (unit * unit), value.astype(F32) * unit])
        key_t = key_f.T.astype(BF)
        state = dot(wide([key_t, key_t]), tall(pieces(right, 2)))
        total = state if total is None else total + state
        if sub + 1 < subs:
            before_ref[sub] = total
    total_ref[...] = without_mirror(total)


def from_others(index, own, others, steps):
    total, earlier = own, None
    for step, ref in zip(steps, others):
        value = ref[...]
        total = total + value
        part = jnp.where(index >= step, value, 0.0)
        earlier = part if earlier is None else earlier + part
    return total, earlier


def row_kernel(own_ref, *refs, steps):
    total_ref, earlier_ref = refs[-2:]
    total, earlier = from_others(
        lax.axis_index("y"), own_ref[...], refs[:-2], steps
    )
    total_ref[...] = total
    earlier_ref[...] = earlier


def prepare_kernel(
    arrived_ref, query_ref, key_t_ref, weight_ref, unit_ref, parts_ref, image_ref, *, subs
):
    row = lax.broadcasted_iota(jnp.int32, (SUB, SUB), 0)
    column = lax.broadcasted_iota(jnp.int32, (SUB, SUB), 1)
    causal = column <= row
    for sub in range(subs):
        key = tokens_of(arrived_ref, 1, sub)
        key_f = key.astype(F32)
        unit = lax.rsqrt(jnp.sum((key_f * key_f).T, 0, keepdims=True) + EPS)
        weight = jnp.where(causal, unit * unit, 0.0)
        unit_ref[sub] = jnp.where(causal, unit, 0.0)
        weight_ref[sub] = weight
        key_t = key_f.T.astype(BF)
        key_t_ref[sub] = key_t
        query = tokens_of(arrived_ref, 0, sub).astype(F32)
        query = query * lax.rsqrt(squared_sum(query) + EPS)
        query_ref[sub] = query
        parts = wide(pieces(query, 3))
        parts_ref[sub] = parts
        scores = dot(parts, tall([key_t] * 3)) * weight
        image_ref[sub] = dot(wide(pieces(scores, 2)), tall([key, key]))


def solve_kernel(
    head_ref, arrived_ref, before_ref, earlier_ref, query_ref, key_t_ref, weight_ref, unit_ref,
    parts_ref, image_ref, *refs, subs, steps
):
    out_ref = refs[-1]
    gain, strength = head_ref[0:1, :], head_ref[1:2, :]
    earlier = earlier_ref[...]
    _, rows_before = from_others(lax.axis_index("x"), earlier, refs[:-1], steps)
    key_base, value_base = with_mirror(earlier + rows_before)

    every = range(subs)
    key_pair, operator, low_state, value_state = [], [], [], []
    resid, answer, direction, rr_now = [], [], [], []
    for sub in every:
        key_state, value = key_base, value_base
        if sub > 0:
            key_state = key_state + before_ref[sub - 1, :, :DH]
            value = value + before_ref[sub - 1, :, DH:]
        high, middle, low = pieces(key_state, 3)
        key = tokens_of(arrived_ref, 1, sub)
        key_pair.append(tall([key, key]))
        line = wide([key_t_ref[sub], high])
        operator.append(tall([line, line, line, wide([jnp.zeros_like(high), middle])]))
        low_state.append(tall([middle, low]))
        value_state.append(value)
        query = query_ref[sub]
        resid.append(query)
        direction.append(query)
        answer.append(None)
        rr_now.append(squared_sum(query))
    def one_turn(s, turn):
        if turn == 0:
            p = [parts_ref[s, :, i * DH : (i + 1) * DH] for i in range(3)]
            image = dot(wide(p + p[:1]), operator[s][:, SUB:]) + image_ref[s]
        else:
            p = pieces(direction[s], 3)
            first = dot(wide(p + p[:1]), operator[s])
            scores = wide(pieces(first[:, :SUB] * weight_ref[s], 2))
            image = dot(scores, key_pair[s]) + first[:, SUB:]
        image = image + dot(wide([p[1], p[0]]), low_state[s]) + strength * direction[s]
        alpha = rr_now[s] / (jnp.sum(direction[s] * image, -1, keepdims=True) + EPS)
        step = alpha * direction[s]
        answer[s] = step if turn == 0 else answer[s] + step
        if turn + 1 < ITERS:
            resid[s] = resid[s] - alpha * image
            rr_next = squared_sum(resid[s])
            direction[s] = resid[s] + rr_next / (rr_now[s] + EPS) * direction[s]
            rr_now[s] = rr_next

    for turn in range(ITERS):
        for s in every:
            one_turn(s, turn)
    parts = [wide(pieces(answer[s], 2)) for s in every]
    split = [pieces(value_state[s], 2) for s in every]
    first = [
        dot(parts[s], tall([wide([key_t_ref[s], split[s][0]])] * 2)) for s in every
    ]
    rest = [dot(parts[s][:, :DH], split[s][1]) for s in every]
    scores = [wide(pieces(first[s][:, :SUB] * unit_ref[s], 2)) for s in every]
    values = [tokens_of(arrived_ref, 2, s) for s in every]
    readout = [
        dot(scores[s], tall([values[s], values[s]])) + (first[s][:, SUB:] + rest[s])
        for s in every
    ]
    rows = out_ref.shape[1]
    count = SUB // rows
    for s in every:
        scale = lax.rsqrt(squared_sum(readout[s]) * (1.0 / DH) + EPS)
        normed = (readout[s] * scale * gain).astype(BF)
        for i in range(count):
            out_ref[s * count + i] = normed[i * rows : (i + 1) * rows]


def exchange(value):
    return lax.all_to_all(value, PEERS, 0, 0, tiled=True)


def from_ring(value, axis, steps):
    size = lax.axis_size(axis)
    return [
        lax.ppermute(value, axis, [(i, (i + step) % size) for i in range(size)]) for step in steps
    ]


def ring_steps(size):
    return [size - 1] + list(range(1, size - 1))


def in_hbm(value):
    return pltpu.with_memory_space_constraint(value, pltpu.HBM)


def on_device(queries, keys, values, ridge, gain):
    rows, columns = queries.shape
    half = lax.axis_size("head")
    peers = 2 * half
    n_x, n_y = lax.axis_size("x"), lax.axis_size("y")
    subs = peers * rows // SUB
    steps_x, steps_y = ring_steps(n_x), ring_steps(n_y)
    packed, head = pl.pallas_call(
        functools.partial(pack_kernel, peers=peers),
        out_shape=(
            jax.ShapeDtypeStruct((peers, 3, rows, DH), BF),
            jax.ShapeDtypeStruct((8, DH), F32),
        ),
        in_specs=[HBM] * 5,
        out_specs=(VMEM, VMEM),
        scratch_shapes=[
            pltpu.VMEM((3, rows, columns), BF),
            pltpu.SMEM((2,), F32),
            pltpu.VMEM((2, DH), F32),
            pltpu.SemaphoreType.DMA((5,)),
        ],
        compiler_params=ROOM,
        name="pack",
    )(*map(in_hbm, (queries, keys, values, ridge, gain.reshape(2, DH))))
    arrived = exchange(packed)

    state = jax.ShapeDtypeStruct((DH + HALF + HALF // 2, DH), F32)
    before, own = pl.pallas_call(
        functools.partial(states_kernel, subs=subs),
        out_shape=(jax.ShapeDtypeStruct((subs - 1, DH, 2 * DH), F32), state),
        in_specs=[VMEM],
        out_specs=(VMEM, VMEM),
        compiler_params=ROOM,
        name="states",
    )(arrived)
    total, earlier = pl.pallas_call(
        functools.partial(row_kernel, steps=steps_y),
        out_shape=(state, state),
        in_specs=[VMEM] * n_y,
        out_specs=(VMEM, VMEM),
        compiler_params=ROOM,
        name="row",
    )(own, *from_ring(own, "y", steps_y))
    square = (subs, SUB, DH)
    prepared = pl.pallas_call(
        functools.partial(prepare_kernel, subs=subs),
        out_shape=(
            jax.ShapeDtypeStruct(square, F32),
            jax.ShapeDtypeStruct(square, BF),
            jax.ShapeDtypeStruct(square, F32),
            jax.ShapeDtypeStruct(square, F32),
            jax.ShapeDtypeStruct((subs, SUB, 3 * DH), BF),
            jax.ShapeDtypeStruct(square, F32),
        ),
        in_specs=[VMEM],
        out_specs=(VMEM,) * 6,
        compiler_params=ROOM,
        name="prepare",
    )(arrived)
    outgoing = pl.pallas_call(
        functools.partial(solve_kernel, subs=subs, steps=steps_x),
        out_shape=jax.ShapeDtypeStruct((peers, rows, DH), BF),
        in_specs=[VMEM] * (9 + n_x),
        out_specs=VMEM,
        compiler_params=ROOM,
        name="solve",
    )(head, arrived, before, earlier, *prepared, *from_ring(total, "x", steps_x))
    return pl.pallas_call(
        unpack_kernel,
        out_shape=jax.ShapeDtypeStruct((rows, columns), BF),
        in_specs=[VMEM],
        out_specs=VMEM,
        compiler_params=ROOM,
        name="unpack",
    )(exchange(outgoing))


def solution(mesh):
    split = Mesh(mesh.devices.reshape(4, 4, 2, mesh.shape["head"]), CTX_HEAD)
    rows = P(CTX_HEAD, None)
    return jax.shard_map(
        on_device,
        mesh=split,
        in_specs=(rows, rows, rows, P("head"), P("head")),
        out_specs=rows,
        check_vma=False,
    )
```

```python
import functools

import jax
import jax.numpy as jnp
from jax import lax
from jax.experimental import pallas as pl
from jax.experimental.pallas import tpu as pltpu
from jax.sharding import Mesh
from jax.sharding import PartitionSpec as P

ITERS = 4
CTX_HEAD = ("x", "y", "core", "head")
PEERS = ("core", "head")
EPS = 1e-06
DH = 128
SUB = 128
HALF = DH // 2

VMEM = pl.BlockSpec(memory_space=pltpu.VMEM)
HBM = pl.BlockSpec(memory_space=pltpu.HBM)
SMEM = pl.BlockSpec(memory_space=pltpu.SMEM)
BF = jnp.bfloat16
F32 = jnp.float32
ROOM = pltpu.CompilerParams(vmem_limit_bytes=16 * 2**20)


def pieces(value, count):
    out = []
    for _ in range(count - 1):
        out.append(value.astype(BF))
        value = value - out[-1].astype(F32)
    return out + [value.astype(BF)]


def wide(parts):
    return jnp.concatenate(parts, 1)


def tall(parts):
    return jnp.concatenate(parts, 0)


def dot(a, b):
    return lax.dot_general(a, b, (((1,), (0,)), ((), ())), preferred_element_type=F32)


def tokens_of(arrived_ref, which, sub):
    count = SUB // arrived_ref.shape[2]
    return tall([arrived_ref[sub * count + i, which] for i in range(count)])


def squared_sum(value):
    return jnp.sum(value * value, -1, keepdims=True)


def pack_kernel(
    query_ref, key_ref, value_ref, ridge_ref, gain_ref, out_ref, head_ref,
    held, ridges, gains, flags, *, peers
):
    half = peers // 2
    copies = [
        pltpu.make_async_copy(source, target, flags.at[i])
        for i, (source, target) in enumerate(
            (
                (query_ref, held.at[0]),
                (key_ref, held.at[1]),
                (value_ref, held.at[2]),
                (ridge_ref, ridges),
                (gain_ref, gains),
            )
        )
    ]
    for copy in copies:
        copy.start()
    for i in range(3):
        copies[i].wait()
        for peer in range(peers):
            head = 2 * (peer % half) + peer // half
            out_ref[peer, i] = held[i, :, head * DH : (head + 1) * DH]
    copies[3].wait()
    copies[4].wait()
    core = lax.axis_index("core")
    head_ref[...] = jnp.full(head_ref.shape, ridges[core], F32)
    head_ref[pl.ds(0, 1), :] = gains[pl.ds(core, 1), :]


def unpack_kernel(arrived_ref, out_ref):
    peers = arrived_ref.shape[0]
    half = peers // 2
    for peer in range(peers):
        head = 2 * (peer % half) + peer // half
        out_ref[:, head * DH : (head + 1) * DH] = arrived_ref[peer]


def without_mirror(state):
    key_state, value_state = state[:, :DH], state[:, DH:]
    corner = key_state[HALF:, HALF:]
    return tall(
        [value_state, key_state[:HALF], wide([corner[: HALF // 2], corner[HALF // 2 :]])]
    )


def with_mirror(rows):
    upper, corner = rows[DH : DH + HALF], rows[DH + HALF :]
    corner = tall([corner[:, :HALF], corner[:, HALF:]])
    lower = wide([upper[:, HALF:].T, corner])
    return tall([upper, lower]), rows[:DH]


def states_kernel(arrived_ref, before_ref, total_ref, *, subs):
    total = None
    for sub in range(subs):
        key = tokens_of(arrived_ref, 1, sub)
        value = tokens_of(arrived_ref, 2, sub)
        key_f = key.astype(F32)
        unit = lax.rsqrt(squared_sum(key_f) + EPS)
        right = wide([key_f * (unit * unit), value.astype(F32) * unit])
        key_t = key_f.T.astype(BF)
        state = dot(wide([key_t, key_t]), tall(pieces(right, 2)))
        total = state if total is None else total + state
        if sub + 1 < subs:
            before_ref[sub] = total
    total_ref[...] = without_mirror(total)


def ring_places():
    core, x, y = lax.axis_index("core"), lax.axis_index("x"), lax.axis_index("y")
    return core == 0, jnp.where(core == 0, y, x), jnp.where(core == 0, x, y)


def gather_kernel(own_ref, *refs, steps, size):
    count = len(steps)
    others, sends, keep_ref = refs[:count], refs[count:-1], refs[-1]
    later_steps = [1, 3, 2]
    by_row, first, second = ring_places()
    own = own_ref[...]
    total, earlier = own, None
    for step, ref in zip(steps, others):
        value = ref[...]
        total = total + value
        part = jnp.where(first >= step, value, 0.0)
        earlier = part if earlier is None else earlier + part
    keep_ref[...] = earlier
    both = earlier + own
    for step, ref in zip(later_steps, sends):
        ref[...] = jnp.where(by_row, total, jnp.where(second + step < size, both, earlier))


def prepare_kernel(
    arrived_ref, query_ref, key_t_ref, weight_ref, unit_ref, parts_ref, image_ref, *, subs
):
    row = lax.broadcasted_iota(jnp.int32, (SUB, SUB), 0)
    column = lax.broadcasted_iota(jnp.int32, (SUB, SUB), 1)
    causal = column <= row
    for sub in range(subs):
        key = tokens_of(arrived_ref, 1, sub)
        key_f = key.astype(F32)
        unit = lax.rsqrt(jnp.sum((key_f * key_f).T, 0, keepdims=True) + EPS)
        weight = jnp.where(causal, unit * unit, 0.0)
        unit_ref[sub] = jnp.where(causal, unit, 0.0)
        weight_ref[sub] = weight
        key_t = key_f.T.astype(BF)
        key_t_ref[sub] = key_t
        query = tokens_of(arrived_ref, 0, sub).astype(F32)
        query = query * lax.rsqrt(squared_sum(query) + EPS)
        query_ref[sub] = query
        parts = wide(pieces(query, 3))
        parts_ref[sub] = parts
        scores = dot(parts, tall([key_t] * 3)) * weight
        image_ref[sub] = dot(wide(pieces(scores, 2)), tall([key, key]))


def solve_kernel(
    head_ref, arrived_ref, before_ref, earlier_ref, query_ref, key_t_ref, weight_ref, unit_ref,
    parts_ref, image_ref, *refs, subs, steps
):
    out_ref = refs[-1]
    gain, strength = head_ref[0:1, :], head_ref[1:2, :]
    by_row, _, second = ring_places()
    earlier = earlier_ref[...]
    for step, ref in zip(steps, refs[:-1]):
        taken = jnp.logical_or(jnp.logical_not(by_row), second >= step)
        earlier = earlier + jnp.where(taken, ref[...], 0.0)
    key_base, value_base = with_mirror(earlier)

    every = range(subs)
    key_pair, operator, low_state, value_state = [], [], [], []
    resid, answer, direction, rr_now = [], [], [], []
    for sub in every:
        key_state, value = key_base, value_base
        if sub > 0:
            key_state = key_state + before_ref[sub - 1, :, :DH]
            value = value + before_ref[sub - 1, :, DH:]
        high, middle, low = pieces(key_state, 3)
        key = tokens_of(arrived_ref, 1, sub)
        key_pair.append(tall([key, key]))
        line = wide([key_t_ref[sub], high])
        operator.append(tall([line, line, line, wide([jnp.zeros_like(high), middle])]))
        low_state.append(tall([middle, low]))
        value_state.append(value)
        query = query_ref[sub]
        resid.append(query)
        direction.append(query)
        answer.append(None)
        rr_now.append(squared_sum(query))
    def one_turn(s, turn):
        if turn == 0:
            p = [parts_ref[s, :, i * DH : (i + 1) * DH] for i in range(3)]
            image = dot(wide(p + p[:1]), operator[s][:, SUB:]) + image_ref[s]
        else:
            p = pieces(direction[s], 3)
            first = dot(wide(p + p[:1]), operator[s])
            scores = wide(pieces(first[:, :SUB] * weight_ref[s], 2))
            image = dot(scores, key_pair[s]) + first[:, SUB:]
        image = image + dot(wide([p[1], p[0]]), low_state[s]) + strength * direction[s]
        alpha = rr_now[s] / (jnp.sum(direction[s] * image, -1, keepdims=True) + EPS)
        step = alpha * direction[s]
        answer[s] = step if turn == 0 else answer[s] + step
        if turn + 1 < ITERS:
            resid[s] = resid[s] - alpha * image
            rr_next = squared_sum(resid[s])
            direction[s] = resid[s] + rr_next / (rr_now[s] + EPS) * direction[s]
            rr_now[s] = rr_next

    for turn in range(ITERS):
        for s in every:
            one_turn(s, turn)
    parts = [wide(pieces(answer[s], 2)) for s in every]
    split = [pieces(value_state[s], 2) for s in every]
    first = [
        dot(parts[s], tall([wide([key_t_ref[s], split[s][0]])] * 2)) for s in every
    ]
    rest = [dot(parts[s][:, :DH], split[s][1]) for s in every]
    scores = [wide(pieces(first[s][:, :SUB] * unit_ref[s], 2)) for s in every]
    values = [tokens_of(arrived_ref, 2, s) for s in every]
    readout = [
        dot(scores[s], tall([values[s], values[s]])) + (first[s][:, SUB:] + rest[s])
        for s in every
    ]
    rows = out_ref.shape[1]
    count = SUB // rows
    for s in every:
        scale = lax.rsqrt(squared_sum(readout[s]) * (1.0 / DH) + EPS)
        normed = (readout[s] * scale * gain).astype(BF)
        for i in range(count):
            out_ref[s * count + i] = normed[i * rows : (i + 1) * rows]


def exchange(value):
    return lax.all_to_all(value, PEERS, 0, 0, tiled=True)


def from_ring(values, steps, size, stage):
    def place(x, y, core):
        return (x * size + y) * 2 + core

    def pairs(step):
        out = []
        for x in range(size):
            for y in range(size):
                for core in range(2):
                    along_y = core == stage
                    to_x = x if along_y else (x + step) % size
                    to_y = (y + step) % size if along_y else y
                    out.append((place(x, y, core), place(to_x, to_y, core)))
        return out

    axes = ("x", "y", "core")
    return [lax.ppermute(value, axes, pairs(step)) for value, step in zip(values, steps)]


def ring_steps(size):
    return [3, 1, 2]


def in_hbm(value):
    return pltpu.with_memory_space_constraint(value, pltpu.HBM)


def on_device(queries, keys, values, ridge, gain):
    rows, columns = queries.shape
    half = lax.axis_size("head")
    peers = 2 * half
    size = lax.axis_size("x")
    subs = peers * rows // SUB
    steps = ring_steps(size)
    packed, head = pl.pallas_call(
        functools.partial(pack_kernel, peers=peers),
        out_shape=(
            jax.ShapeDtypeStruct((peers, 3, rows, DH), BF),
            jax.ShapeDtypeStruct((8, DH), F32),
        ),
        in_specs=[HBM] * 5,
        out_specs=(VMEM, VMEM),
        scratch_shapes=[
            pltpu.VMEM((3, rows, columns), BF),
            pltpu.SMEM((2,), F32),
            pltpu.VMEM((2, DH), F32),
            pltpu.SemaphoreType.DMA((5,)),
        ],
        compiler_params=ROOM,
        name="pack",
    )(*map(in_hbm, (queries, keys, values, ridge, gain.reshape(2, DH))))
    arrived = exchange(packed)

    state = jax.ShapeDtypeStruct((DH + HALF + HALF // 2, DH), F32)
    before, own = pl.pallas_call(
        functools.partial(states_kernel, subs=subs),
        out_shape=(jax.ShapeDtypeStruct((subs - 1, DH, 2 * DH), F32), state),
        in_specs=[VMEM],
        out_specs=(VMEM, VMEM),
        compiler_params=ROOM,
        name="states",
    )(arrived)
    square = (subs, SUB, DH)
    prepared = pl.pallas_call(
        functools.partial(prepare_kernel, subs=subs),
        out_shape=(
            jax.ShapeDtypeStruct(square, F32),
            jax.ShapeDtypeStruct(square, BF),
            jax.ShapeDtypeStruct(square, F32),
            jax.ShapeDtypeStruct(square, F32),
            jax.ShapeDtypeStruct((subs, SUB, 3 * DH), BF),
            jax.ShapeDtypeStruct(square, F32),
        ),
        in_specs=[VMEM],
        out_specs=(VMEM,) * 6,
        compiler_params=ROOM,
        name="prepare",
    )(arrived)
    around, prepared = lax.optimization_barrier(
        (from_ring([own] * len(steps), steps, size, 0), prepared)
    )
    *sends, keep = pl.pallas_call(
        functools.partial(gather_kernel, steps=steps, size=size),
        out_shape=(state,) * size,
        in_specs=[VMEM] * size,
        out_specs=(VMEM,) * size,
        compiler_params=ROOM,
        name="gather",
    )(own, *around)
    outgoing = pl.pallas_call(
        functools.partial(solve_kernel, subs=subs, steps=[1, 3, 2]),
        out_shape=jax.ShapeDtypeStruct((peers, rows, DH), BF),
        in_specs=[VMEM] * (9 + size),
        out_specs=VMEM,
        compiler_params=ROOM,
        name="solve",
    )(head, arrived, before, keep, *prepared, *from_ring(sends, [1, 3, 2], size, 1))
    return pl.pallas_call(
        unpack_kernel,
        out_shape=jax.ShapeDtypeStruct((rows, columns), BF),
        in_specs=[VMEM],
        out_specs=VMEM,
        compiler_params=ROOM,
        name="unpack",
    )(exchange(outgoing))


def solution(mesh):
    split = Mesh(mesh.devices.reshape(4, 4, 2, mesh.shape["head"]), CTX_HEAD)
    rows = P(CTX_HEAD, None)
    return jax.shard_map(
        on_device,
        mesh=split,
        in_specs=(rows, rows, rows, P("head"), P("head")),
        out_specs=rows,
        check_vma=False,
    )
```

```python
import functools

import jax
import jax.numpy as jnp
from jax import lax
from jax.experimental import pallas as pl
from jax.experimental.pallas import tpu as pltpu
from jax.sharding import Mesh
from jax.sharding import PartitionSpec as P

ITERS = 4
CTX_HEAD = ("x", "y", "core", "head")
PEERS = ("core", "head")
EPS = 1e-06
DH = 128
SUB = 128
HALF = DH // 2

VMEM = pl.BlockSpec(memory_space=pltpu.VMEM)
HBM = pl.BlockSpec(memory_space=pltpu.HBM)
SMEM = pl.BlockSpec(memory_space=pltpu.SMEM)
BF = jnp.bfloat16
F32 = jnp.float32
ROOM = pltpu.CompilerParams(vmem_limit_bytes=16 * 2**20)


def pieces(value, count):
    out = []
    for _ in range(count - 1):
        out.append(value.astype(BF))
        value = value - out[-1].astype(F32)
    return out + [value.astype(BF)]


def wide(parts):
    return jnp.concatenate(parts, 1)


def tall(parts):
    return jnp.concatenate(parts, 0)


def dot(a, b):
    return lax.dot_general(a, b, (((1,), (0,)), ((), ())), preferred_element_type=F32)


def tokens_of(arrived_ref, which, sub):
    count = SUB // arrived_ref.shape[2]
    return tall([arrived_ref[sub * count + i, which] for i in range(count)])


def squared_sum(value):
    return jnp.sum(value * value, -1, keepdims=True)


def pack_kernel(
    query_ref, key_ref, value_ref, ridge_ref, gain_ref, out_ref, head_ref,
    held, ridges, gains, flags, *, peers
):
    half = peers // 2
    copies = [
        pltpu.make_async_copy(source, target, flags.at[i])
        for i, (source, target) in enumerate(
            (
                (query_ref, held.at[0]),
                (key_ref, held.at[1]),
                (value_ref, held.at[2]),
                (ridge_ref, ridges),
                (gain_ref, gains),
            )
        )
    ]
    for copy in copies:
        copy.start()
    for i in range(3):
        copies[i].wait()
        for peer in range(peers):
            head = 2 * (peer % half) + peer // half
            out_ref[peer, i] = held[i, :, head * DH : (head + 1) * DH]
    copies[3].wait()
    copies[4].wait()
    core = lax.axis_index("core")
    head_ref[...] = jnp.full(head_ref.shape, ridges[core], F32)
    head_ref[pl.ds(0, 1), :] = gains[pl.ds(core, 1), :]


def unpack_kernel(arrived_ref, out_ref):
    peers = arrived_ref.shape[0]
    half = peers // 2
    for peer in range(peers):
        head = 2 * (peer % half) + peer // half
        out_ref[:, head * DH : (head + 1) * DH] = arrived_ref[peer]


def without_mirror(state):
    key_state, value_state = state[:, :DH], state[:, DH:]
    corner = key_state[HALF:, HALF:]
    return tall(
        [value_state, key_state[:HALF], wide([corner[: HALF // 2], corner[HALF // 2 :]])]
    )


def with_mirror(rows):
    upper, corner = rows[DH : DH + HALF], rows[DH + HALF :]
    corner = tall([corner[:, :HALF], corner[:, HALF:]])
    lower = wide([upper[:, HALF:].T, corner])
    return tall([upper, lower]), rows[:DH]


def state_of(arrived_ref, sub):
    key_f = tokens_of(arrived_ref, 1, sub).astype(F32)
    unit = lax.rsqrt(squared_sum(key_f) + EPS)
    right = wide(
        [key_f * (unit * unit), tokens_of(arrived_ref, 2, sub).astype(F32) * unit]
    )
    key_t = key_f.T.astype(BF)
    return dot(wide([key_t, key_t]), tall(pieces(right, 2)))


def states_kernel(arrived_ref, total_ref, *, subs):
    total = state_of(arrived_ref, 0)
    for sub in range(1, subs):
        total = total + state_of(arrived_ref, sub)
    total_ref[...] = without_mirror(total)


def ring_places():
    core, x, y = lax.axis_index("core"), lax.axis_index("x"), lax.axis_index("y")
    return core == 0, jnp.where(core == 0, y, x), jnp.where(core == 0, x, y)


def gather_kernel(own_ref, *refs, steps, size):
    count = len(steps)
    others, sends, keep_ref = refs[:count], refs[count:-1], refs[-1]
    later_steps = [1, 3, 2]
    by_row, first, second = ring_places()
    own = own_ref[...]
    total, earlier = own, None
    for step, ref in zip(steps, others):
        value = ref[...]
        total = total + value
        part = jnp.where(first >= step, value, 0.0)
        earlier = part if earlier is None else earlier + part
    keep_ref[...] = earlier
    both = earlier + own
    for step, ref in zip(later_steps, sends):
        ref[...] = jnp.where(by_row, total, jnp.where(second + step < size, both, earlier))


def prepare_kernel(
    arrived_ref, before_ref, query_ref, key_t_ref, weight_ref, unit_ref, parts_ref, image_ref,
    *, subs
):
    row = lax.broadcasted_iota(jnp.int32, (SUB, SUB), 0)
    column = lax.broadcasted_iota(jnp.int32, (SUB, SUB), 1)
    causal = column <= row
    total = None
    for sub in range(subs):
        if sub + 1 < subs:
            state = state_of(arrived_ref, sub)
            total = state if sub == 0 else total + state
            before_ref[sub] = total
        key = tokens_of(arrived_ref, 1, sub)
        key_f = key.astype(F32)
        unit = lax.rsqrt(jnp.sum((key_f * key_f).T, 0, keepdims=True) + EPS)
        weight = jnp.where(causal, unit * unit, 0.0)
        unit_ref[sub] = jnp.where(causal, unit, 0.0)
        weight_ref[sub] = weight
        key_t = key_f.T.astype(BF)
        key_t_ref[sub] = key_t
        query = tokens_of(arrived_ref, 0, sub).astype(F32)
        query = query * lax.rsqrt(squared_sum(query) + EPS)
        query_ref[sub] = query
        parts = wide(pieces(query, 3))
        parts_ref[sub] = parts
        scores = dot(parts, tall([key_t] * 3)) * weight
        image_ref[sub] = dot(wide(pieces(scores, 2)), tall([key, key]))


def solve_kernel(
    head_ref, arrived_ref, before_ref, earlier_ref, query_ref, key_t_ref, weight_ref, unit_ref,
    parts_ref, image_ref, *refs, subs, steps
):
    out_ref = refs[-1]
    gain, strength = head_ref[0:1, :], head_ref[1:2, :]
    by_row, _, second = ring_places()
    earlier = earlier_ref[...]
    for step, ref in zip(steps, refs[:-1]):
        taken = jnp.logical_or(jnp.logical_not(by_row), second >= step)
        earlier = earlier + jnp.where(taken, ref[...], 0.0)
    key_base, value_base = with_mirror(earlier)

    every = range(subs)
    key_pair, operator, low_state, value_state = [], [], [], []
    resid, answer, direction, rr_now = [], [], [], []
    for sub in every:
        key_state, value = key_base, value_base
        if sub > 0:
            key_state = key_state + before_ref[sub - 1, :, :DH]
            value = value + before_ref[sub - 1, :, DH:]
        high, middle, low = pieces(key_state, 3)
        key = tokens_of(arrived_ref, 1, sub)
        key_pair.append(tall([key, key]))
        line = wide([key_t_ref[sub], high])
        operator.append(tall([line, line, line, wide([jnp.zeros_like(high), middle])]))
        low_state.append(tall([middle, low]))
        value_state.append(value)
        query = query_ref[sub]
        resid.append(query)
        direction.append(query)
        answer.append(None)
        rr_now.append(squared_sum(query))
    def one_turn(s, turn):
        if turn == 0:
            p = [parts_ref[s, :, i * DH : (i + 1) * DH] for i in range(3)]
            image = dot(wide(p + p[:1]), operator[s][:, SUB:]) + image_ref[s]
        else:
            p = pieces(direction[s], 3)
            first = dot(wide(p + p[:1]), operator[s])
            scores = wide(pieces(first[:, :SUB] * weight_ref[s], 2))
            image = dot(scores, key_pair[s]) + first[:, SUB:]
        image = image + dot(wide([p[1], p[0]]), low_state[s]) + strength * direction[s]
        alpha = rr_now[s] / (jnp.sum(direction[s] * image, -1, keepdims=True) + EPS)
        step = alpha * direction[s]
        answer[s] = step if turn == 0 else answer[s] + step
        if turn + 1 < ITERS:
            resid[s] = resid[s] - alpha * image
            rr_next = squared_sum(resid[s])
            direction[s] = resid[s] + rr_next / (rr_now[s] + EPS) * direction[s]
            rr_now[s] = rr_next

    for turn in range(ITERS):
        for s in every:
            one_turn(s, turn)
    parts = [wide(pieces(answer[s], 2)) for s in every]
    split = [pieces(value_state[s], 2) for s in every]
    first = [
        dot(parts[s], tall([wide([key_t_ref[s], split[s][0]])] * 2)) for s in every
    ]
    rest = [dot(parts[s][:, :DH], split[s][1]) for s in every]
    scores = [wide(pieces(first[s][:, :SUB] * unit_ref[s], 2)) for s in every]
    values = [tokens_of(arrived_ref, 2, s) for s in every]
    readout = [
        dot(scores[s], tall([values[s], values[s]])) + (first[s][:, SUB:] + rest[s])
        for s in every
    ]
    rows = out_ref.shape[1]
    count = SUB // rows
    for s in every:
        scale = lax.rsqrt(squared_sum(readout[s]) * (1.0 / DH) + EPS)
        normed = (readout[s] * scale * gain).astype(BF)
        for i in range(count):
            out_ref[s * count + i] = normed[i * rows : (i + 1) * rows]


def exchange(value):
    return lax.all_to_all(value, PEERS, 0, 0, tiled=True)


def from_ring(values, steps, size, stage):
    def place(x, y, core):
        return (x * size + y) * 2 + core

    def pairs(step):
        out = []
        for x in range(size):
            for y in range(size):
                for core in range(2):
                    along_y = core == stage
                    to_x = x if along_y else (x + step) % size
                    to_y = (y + step) % size if along_y else y
                    out.append((place(x, y, core), place(to_x, to_y, core)))
        return out

    axes = ("x", "y", "core")
    return [lax.ppermute(value, axes, pairs(step)) for value, step in zip(values, steps)]


def ring_steps(size):
    return [3, 1, 2]


def in_hbm(value):
    return pltpu.with_memory_space_constraint(value, pltpu.HBM)


def on_device(queries, keys, values, ridge, gain):
    rows, columns = queries.shape
    half = lax.axis_size("head")
    peers = 2 * half
    size = lax.axis_size("x")
    subs = peers * rows // SUB
    steps = ring_steps(size)
    packed, head = pl.pallas_call(
        functools.partial(pack_kernel, peers=peers),
        out_shape=(
            jax.ShapeDtypeStruct((peers, 3, rows, DH), BF),
            jax.ShapeDtypeStruct((8, DH), F32),
        ),
        in_specs=[HBM] * 5,
        out_specs=(VMEM, VMEM),
        scratch_shapes=[
            pltpu.VMEM((3, rows, columns), BF),
            pltpu.SMEM((2,), F32),
            pltpu.VMEM((2, DH), F32),
            pltpu.SemaphoreType.DMA((5,)),
        ],
        compiler_params=ROOM,
        name="pack",
    )(*map(in_hbm, (queries, keys, values, ridge, gain.reshape(2, DH))))
    arrived = exchange(packed)

    state = jax.ShapeDtypeStruct((DH + HALF + HALF // 2, DH), F32)
    own = pl.pallas_call(
        functools.partial(states_kernel, subs=subs),
        out_shape=state,
        in_specs=[VMEM],
        out_specs=VMEM,
        compiler_params=ROOM,
        name="states",
    )(arrived)
    square = (subs, SUB, DH)
    before, *prepared = pl.pallas_call(
        functools.partial(prepare_kernel, subs=subs),
        out_shape=(
            jax.ShapeDtypeStruct((subs - 1, DH, 2 * DH), F32),
            jax.ShapeDtypeStruct(square, F32),
            jax.ShapeDtypeStruct(square, BF),
            jax.ShapeDtypeStruct(square, F32),
            jax.ShapeDtypeStruct(square, F32),
            jax.ShapeDtypeStruct((subs, SUB, 3 * DH), BF),
            jax.ShapeDtypeStruct(square, F32),
        ),
        in_specs=[VMEM],
        out_specs=(VMEM,) * 7,
        compiler_params=ROOM,
        name="prepare",
    )(arrived)
    around, prepared = lax.optimization_barrier(
        (from_ring([own] * len(steps), steps, size, 0), prepared)
    )
    *sends, keep = pl.pallas_call(
        functools.partial(gather_kernel, steps=steps, size=size),
        out_shape=(state,) * size,
        in_specs=[VMEM] * size,
        out_specs=(VMEM,) * size,
        compiler_params=ROOM,
        name="gather",
    )(own, *around)
    outgoing = pl.pallas_call(
        functools.partial(solve_kernel, subs=subs, steps=[1, 3, 2]),
        out_shape=jax.ShapeDtypeStruct((peers, rows, DH), BF),
        in_specs=[VMEM] * (9 + size),
        out_specs=VMEM,
        compiler_params=ROOM,
        name="solve",
    )(head, arrived, before, keep, *prepared, *from_ring(sends, [1, 3, 2], size, 1))
    return pl.pallas_call(
        unpack_kernel,
        out_shape=jax.ShapeDtypeStruct((rows, columns), BF),
        in_specs=[VMEM],
        out_specs=VMEM,
        compiler_params=ROOM,
        name="unpack",
    )(exchange(outgoing))


def solution(mesh):
    split = Mesh(mesh.devices.reshape(4, 4, 2, mesh.shape["head"]), CTX_HEAD)
    rows = P(CTX_HEAD, None)
    return jax.shard_map(
        on_device,
        mesh=split,
        in_specs=(rows, rows, rows, P("head"), P("head")),
        out_specs=rows,
        check_vma=False,
    )
```
